32 devices in a mesh: blk: 16 (over z, x, core), strip: 2 (over y).
Axes of the slice: x: 2, y: 2, z: 4, core: 2. Of those that a mesh axis runs over, the one named last changes fastest.
Arguments:
- points: bfloat16 [20480, 64], P(('blk', 'strip')), may hold values from -6 to 6
- task_ids: int32 [20480], P(('blk', 'strip')), may hold values from 0 to 3
- rhs: bfloat16 [20480, 32], P(('blk', 'strip')), may hold values from -6 to 6
- length_scales: float32 [64], replicated, may hold values from 2 to 5
- coregion: float32 [4, 4], replicated, may hold values from -4 to 6, as said below
- noise: float32 [1], replicated, may hold values from 0.2 to 1
Outputs:
- product: float32 [20480, 32], P(('blk', 'strip'))
The draws below stay inside these ranges and needn't reach their ends.
Inputs may be any that keep to these rules, and one draw needn't show every extreme that they name: coregion is symmetric positive definite.
All inputs are finite; a program needn't handle non-finite values.
Results may differ from the reference program's by a relative error of at most 0.0041.
Values may be sent and summed in bfloat16 or wider, within the bound.
A program may use at most 64 MiB of HBM per device.

```python
import math
import jax
import jax.numpy as jnp
from jax import lax

FEAT = 64
RHS = 32
TASKS = 4
BLK_PTS = 1280
POINTS = 20480
N_BLK = 16


def draw_coregion(key, part):
    first, second = jax.random.split(jax.random.fold_in(key, 11))
    loading = jnp.clip(jax.random.normal(first, (TASKS, TASKS), jnp.float32), -2.0, 2.0) * 0.5
    extra = jax.random.uniform(second, (TASKS,), jnp.float32, 0.5, 1.5)
    return jnp.dot(loading, loading.T, precision=lax.Precision.HIGHEST) + jnp.diag(extra)


def touch_ends(array, key, least, high):
    place = [jax.random.randint(jax.random.fold_in(key, axis), (), 0, length) for axis, length in enumerate(array.shape)]
    widest = array.shape.index(max(array.shape))
    next_to = place[:widest] + [(place[widest] + 1) % array.shape[widest]] + place[widest + 1:]
    return array.at[tuple(place)].set(least).at[tuple(next_to)].set(high)


def block_scale(rng, shape, cuts, least, top_value):
    gain = 1.0
    for position, shards_of in cuts:
        steps = jax.random.uniform(jax.random.fold_in(jax.random.fold_in(rng, 6), position), (shards_of,), jnp.float32, least / len(cuts), top_value / len(cuts))
        gain = gain * jnp.repeat(jnp.exp(steps), shape[position] // shards_of).reshape((-1,) + (1,) * (len(shape) - 1 - position))
    return gain


def gaussian(own_key, extent, deviation, bound, cuts=(), held_as=jnp.bfloat16):
    level = block_scale(own_key, extent, cuts, -0.22, 0.18) if cuts else 1.0
    values = jax.random.normal(own_key, extent, jnp.float32) * deviation * level
    return jnp.minimum(jnp.maximum(values, -bound), bound).astype(held_as)


def setup_inputs(seed: int = 0) -> dict:
    keys = jax.random.split(jax.random.key(seed), 7)
    points = gaussian(keys[0], (POINTS, FEAT), 1.0, 6.0, ((0, 32),))
    task_ids = touch_ends(jax.random.randint(keys[1], (POINTS,), 0, TASKS), jax.random.fold_in(keys[1], 1), 0, TASKS - 1).astype(jnp.int32)
    rhs = gaussian(keys[2], (POINTS, RHS), 1.0, 6.0, ((0, 32),))
    length_scales = jnp.clip(jnp.exp(jax.random.uniform(keys[3], (FEAT,), jnp.float32, math.log(2.0), math.log(5.0))), 2.0, 5.0)
    coregion = draw_coregion(jax.random.fold_in(keys[6], 71), 0)
    noise = jnp.clip(jax.random.uniform(keys[5], (1,), jnp.float32, 0.2, 1.0), 0.2, 1.0)
    return dict(points=points, task_ids=task_ids, rhs=rhs, length_scales=length_scales, coregion=coregion, noise=noise)


def reference(points, task_ids, rhs, length_scales, coregion, noise):
    scaled = (points.astype(jnp.float32) / length_scales[None, :]).astype(jnp.bfloat16)
    widened = lax.optimization_barrier(scaled).astype(jnp.float32)
    norms = lax.optimization_barrier(jnp.sum(widened * widened, axis=1))
    rhs_wide = rhs.astype(jnp.float32)
    row_factors = coregion[task_ids]
    row_step = BLK_PTS // 4

    def one_block(start):
        rows = lax.dynamic_slice_in_dim(widened, start, row_step, 0)
        row_norms = lax.dynamic_slice_in_dim(norms, start, row_step, 0)
        factors = lax.dynamic_slice_in_dim(row_factors, start, row_step, 0)
        crossed = jnp.dot(rows, widened.T, precision=lax.Precision.HIGHEST)
        squared = jnp.maximum(row_norms[:, None] + norms[None, :] - 2.0 * crossed, 0.0)
        radius = jnp.sqrt(5.0 * squared)
        factor = factors[:, task_ids]
        shaped = (1.0 + radius + radius * radius / 3.0) * jnp.exp(-radius)
        kernel = (factor * shaped).astype(jnp.bfloat16)
        kernel_wide = lax.optimization_barrier(kernel).astype(jnp.float32)
        return jnp.dot(kernel_wide, rhs_wide, precision=lax.Precision.HIGHEST)
    starts = jnp.arange(4 * N_BLK, dtype=jnp.int32) * row_step
    blocks = lax.map(one_block, starts)
    return blocks.reshape(POINTS, RHS) + noise[0] * rhs_wide
```

```python
import functools
import math

import jax
import jax.numpy as jnp
import numpy as np
from jax import lax
from jax.experimental import pallas as pl
from jax.experimental.pallas import tpu as pltpu
from jax.sharding import PartitionSpec as P

MESH = pl.DeviceIdType.MESH
LANES = 128
PIECES = 3


def rounded(value):
    return lax.reduce_precision(value, 8, 7)


def split_f32(value):
    parts = []
    for _ in range(PIECES):
        top = rounded(value)
        parts.append(top.astype(jnp.bfloat16))
        value = value - top
    return parts


def low_size(n_blk, n_strip):
    for size in range(1, n_blk + 1):
        if n_blk % size == 0 and size * n_strip >= n_blk // size:
            return size
    return n_blk


class Sizes:
    def __init__(self, feat, tasks, width):
        self.feat, self.tasks, self.width = feat, tasks, width
        self.norm = feat
        self.one = feat + PIECES
        self.hot = feat + 2 * PIECES
        self.rhs = LANES - width


def constant_mats(s):
    swap = np.zeros((LANES, LANES), np.float32)
    for i in range(s.feat):
        swap[i, i] = -2.0
    for i in range(PIECES):
        swap[s.one + i, s.norm + i] = 1.0
        swap[s.norm + i, s.one + i] = 1.0
    hots = np.zeros((LANES, LANES), np.float32)
    vals = np.zeros((LANES, LANES), np.float32)
    for t in range(s.tasks):
        for c in range(s.width):
            hots[s.hot + t, t * s.width + c] = 1.0
            vals[s.rhs + c, t * s.width + c] = 1.0
    return jnp.asarray(np.stack([swap, hots, vals]), jnp.bfloat16)


def pack_points(points, task_ids, rhs, length_scales, s):
    n = points.shape[0]
    scaled = rounded(points.astype(jnp.float32) / length_scales[None, :])
    norms = jnp.sum(scaled * scaled, axis=1, keepdims=True)
    hot = task_ids[:, None] == jnp.arange(s.tasks, dtype=jnp.int32)[None, :]
    blank = jnp.zeros((n, s.rhs - s.hot - s.tasks), jnp.bfloat16)
    return jnp.concatenate(
        [
            scaled.astype(jnp.bfloat16),
            *split_f32(norms),
            jnp.ones((n, PIECES), jnp.bfloat16),
            hot.astype(jnp.bfloat16),
            blank,
            rhs,
        ],
        axis=1,
    )


def factor_mats(coregion, s):
    wide = jnp.repeat(coregion * jnp.float32(5.0 / 3.0), s.width, axis=1)
    wide = jnp.pad(wide, ((s.hot, LANES - s.hot - s.tasks), (0, LANES - s.tasks * s.width)))
    return jnp.stack(split_f32(wide))


def shaped_times(left, right, values):
    squared = lax.dot_general(
        left, right, (((1,), (1,)), ((), ())), preferred_element_type=jnp.float32
    )
    squared = jnp.maximum(squared, 1e-30)
    root = squared * lax.rsqrt(squared)
    decay = jnp.exp2(root * (-math.sqrt(5.0) / math.log(2.0)))
    shaped = ((squared + 0.6) + root * (3.0 / math.sqrt(5.0))) * decay
    return jnp.dot(shaped.astype(jnp.bfloat16), values, preferred_element_type=jnp.float32)


def kernel(
    s, low, n_strip, high, group,
    x_ref, mats_ref, factors_ref, noise_ref, out_ref,
    rows, cols, col_w, col_r, sums, outbox, inbox,
    row_send, row_recv, col_send, col_recv, sum_send, sum_recv,
):
    n = x_ref.shape[0]
    n_a, n_b = low * n_strip, high
    tm = math.gcd(n, 128)
    blk, strip = lax.axis_index("blk"), lax.axis_index("strip")
    mine_b, mine_a = blk // low, (blk % low) * n_strip + strip

    def peer_a(index):
        return (mine_b * low + index // n_strip, index % n_strip)

    def peer_b(index):
        return (index * low + blk % low, strip)

    barrier = pltpu.get_barrier_semaphore()
    for k in range(1, n_a):
        pl.semaphore_signal(
            barrier, inc=1, device_id=peer_a((mine_a + k) % n_a), device_id_type=MESH
        )
    for k in range(1, n_b):
        pl.semaphore_signal(
            barrier, inc=1, device_id=peer_b((mine_b + k) % n_b), device_id_type=MESH
        )
    pl.semaphore_wait(barrier, n_a + n_b - 2)

    def col_copy(k):
        return pltpu.make_async_remote_copy(
            src_ref=x_ref, dst_ref=cols.at[k],
            send_sem=col_send.at[k], recv_sem=col_recv.at[k],
            device_id=peer_b((mine_b + k) % n_b), device_id_type=MESH,
        )

    def row_copy(k):
        return pltpu.make_async_remote_copy(
            src_ref=x_ref, dst_ref=rows.at[k],
            send_sem=row_send.at[k], recv_sem=row_recv.at[k],
            device_id=peer_a((mine_a + k) % n_a), device_id_type=MESH,
        )

    def sum_copy(k):
        return pltpu.make_async_remote_copy(
            src_ref=outbox.at[k], dst_ref=inbox.at[k],
            send_sem=sum_send.at[k], recv_sem=sum_recv.at[k],
            device_id=peer_a((mine_a + n_a - k) % n_a), device_id_type=MESH,
        )

    for k in range(1, max(n_a, n_b)):
        if k < n_b:
            col_copy(k).start()
        if k < n_a:
            row_copy(k).start()

    rows[0] = x_ref[...]
    cols[0] = x_ref[...]
    phases = n_b // group

    def phase(ph, _):
        for g in range(group):
            k = ph * group + g

            @pl.when(k > 0)
            def _():
                col_copy(k).wait_recv()

            block = cols[k]
            place = pl.ds(pl.multiple_of(k * n, 32), n)
            col_w[place, :] = jnp.dot(
                block, mats_ref[0], preferred_element_type=jnp.float32
            ).astype(jnp.bfloat16)
            hots = jnp.dot(block, mats_ref[1], preferred_element_type=jnp.float32)
            vals = jnp.dot(block, mats_ref[2], preferred_element_type=jnp.float32)
            col_r[place, :] = (hots * vals).astype(jnp.bfloat16)

        window = pl.ds(pl.multiple_of(ph * (group * n), 32), group * n)

        def row_block(a, _):
            @pl.when(jnp.logical_and(ph == 0, a > 0))
            def _():
                row_copy(a).wait_recv()

            def chunk(i, _):
                at = pl.ds(pl.multiple_of(i * tm, tm), tm)
                got = shaped_times(rows[a, at, :], col_w[window, :], col_r[window, :])

                @pl.when(ph == 0)
                def _():
                    sums[a, at, :] = got

                @pl.when(ph > 0)
                def _():
                    sums[a, at, :] = sums[a, at, :] + got

                return 0

            lax.fori_loop(0, n // tm, chunk, 0)

            @pl.when(ph == phases - 1)
            def _():
                block = rows[a]
                factor = jnp.dot(block, factors_ref[0], preferred_element_type=jnp.float32)
                for piece in range(1, PIECES):
                    factor = factor + jnp.dot(
                        block, factors_ref[piece], preferred_element_type=jnp.float32
                    )
                total = sums[a] * factor
                turn = s.width
                while turn < LANES:
                    total = total + pltpu.roll(total, turn, 1)
                    turn *= 2
                part = n // s.tasks
                lane = lax.broadcasted_iota(jnp.int32, (part, LANES), 1)
                packed = total[:part]
                for t in range(1, s.tasks):
                    packed = jnp.where(lane >= t * s.width, total[t * part:(t + 1) * part], packed)
                outbox[a] = packed

                @pl.when(a > 0)
                def _():
                    sum_copy(a).start()

            return 0

        lax.fori_loop(0, n_a, row_block, 0)
        return 0

    lax.fori_loop(0, phases, phase, 0)
    for k in range(1, n_b):
        col_copy(k).wait_send()
    for k in range(1, n_a):
        row_copy(k).wait_send()
    total = outbox[0]
    for k in range(1, n_a):
        sum_copy(k).wait_recv()
        total = total + inbox[k]
    part = n // s.tasks
    for t in range(s.tasks):
        span = slice(t * part, (t + 1) * part)
        out_ref[span, :] = (
            total[:, t * s.width:(t + 1) * s.width]
            + noise_ref[0] * x_ref[span, s.rhs:].astype(jnp.float32)
        )
    for k in range(1, n_a):
        sum_copy(k).wait_send()


def solution(mesh):
    n_blk, n_strip = mesh.shape["blk"], mesh.shape["strip"]
    low = low_size(n_blk, n_strip)
    high = n_blk // low
    n_a, n_b = low * n_strip, high
    group = 2 if n_b % 2 == 0 else 1

    def body(points, task_ids, rhs, length_scales, coregion, noise):
        n = points.shape[0]
        s = Sizes(points.shape[1], coregion.shape[0], rhs.shape[1])
        packed = pack_points(points, task_ids, rhs, length_scales, s)
        vmem = pl.BlockSpec(memory_space=pltpu.VMEM)
        bf16, f32 = jnp.bfloat16, jnp.float32
        return pl.pallas_call(
            functools.partial(kernel, s, low, n_strip, high, group),
            out_shape=jax.ShapeDtypeStruct((n, s.width), f32),
            in_specs=[vmem, vmem, vmem, pl.BlockSpec(memory_space=pltpu.SMEM)],
            out_specs=vmem,
            scratch_shapes=[
                pltpu.VMEM((n_a, n, LANES), bf16),
                pltpu.VMEM((n_b, n, LANES), bf16),
                pltpu.VMEM((n_b * n, LANES), bf16),
                pltpu.VMEM((n_b * n, LANES), bf16),
                pltpu.VMEM((n_a, n, LANES), f32),
                pltpu.VMEM((n_a, n // s.tasks, LANES), f32),
                pltpu.VMEM((n_a, n // s.tasks, LANES), f32),
                pltpu.SemaphoreType.DMA((n_a,)),
                pltpu.SemaphoreType.DMA((n_a,)),
                pltpu.SemaphoreType.DMA((n_b,)),
                pltpu.SemaphoreType.DMA((n_b,)),
                pltpu.SemaphoreType.DMA((n_a,)),
                pltpu.SemaphoreType.DMA((n_a,)),
            ],
            compiler_params=pltpu.CompilerParams(
                collective_id=0, has_side_effects=True, vmem_limit_bytes=60000 * 1024
            ),
        )(packed, constant_mats(s), factor_mats(coregion, s), noise)

    return jax.shard_map(
        body,
        mesh=mesh,
        in_specs=(
            P(("blk", "strip"), None),
            P(("blk", "strip")),
            P(("blk", "strip"), None),
            P(),
            P(),
            P(),
        ),
        out_specs=P(("blk", "strip"), None),
        check_vma=False,
    )
```

```python
import functools
import math

import jax
import jax.numpy as jnp
import numpy as np
from jax import lax
from jax.experimental import pallas as pl
from jax.experimental.pallas import tpu as pltpu
from jax.sharding import PartitionSpec as P

MESH = pl.DeviceIdType.MESH
LANES = 128
NT = (((1,), (1,)), ((), ()))
PIECES = 3


def rounded(value):
    return lax.reduce_precision(value, 8, 7)


def split_f32(value):
    parts = []
    for _ in range(PIECES):
        top = rounded(value)
        parts.append(top.astype(jnp.bfloat16))
        value = value - top
    return parts


def low_size(n_blk, n_strip):
    for size in range(1, n_blk + 1):
        if n_blk % size == 0 and size * n_strip >= n_blk // size:
            return size
    return n_blk


class Sizes:
    def __init__(self, feat, tasks, width):
        self.feat, self.tasks, self.width = feat, tasks, width
        self.norm = feat
        self.one = feat + PIECES
        self.hot = feat + 2 * PIECES
        self.rhs = LANES - width


def constant_mats(s):
    swap = np.zeros((LANES, LANES), np.float32)
    for i in range(s.feat):
        swap[i, i] = -2.0
    for i in range(PIECES):
        swap[s.one + i, s.norm + i] = 1.0
        swap[s.norm + i, s.one + i] = 1.0
    hots = np.zeros((LANES, LANES), np.float32)
    vals = np.zeros((LANES, LANES), np.float32)
    for t in range(s.tasks):
        for c in range(s.width):
            hots[s.hot + t, t * s.width + c] = 1.0
            vals[s.rhs + c, t * s.width + c] = 1.0
    return jnp.asarray(np.stack([swap, hots, vals, hots.T, vals.T]), jnp.bfloat16)


def pack_points(points, task_ids, rhs, length_scales, s):
    n = points.shape[0]
    scaled = rounded(points.astype(jnp.float32) / length_scales[None, :])
    norms = jnp.sum(scaled * scaled, axis=1, keepdims=True)
    hot = task_ids[:, None] == jnp.arange(s.tasks, dtype=jnp.int32)[None, :]
    blank = jnp.zeros((n, s.rhs - s.hot - s.tasks), jnp.bfloat16)
    return jnp.concatenate(
        [
            scaled.astype(jnp.bfloat16),
            *split_f32(norms),
            jnp.ones((n, PIECES), jnp.bfloat16),
            hot.astype(jnp.bfloat16),
            blank,
            rhs,
        ],
        axis=1,
    )


def factor_mats(coregion, s):
    wide = jnp.repeat(coregion * jnp.float32(5.0 / 3.0), s.width, axis=1)
    wide = jnp.pad(wide, ((s.hot, LANES - s.hot - s.tasks), (0, LANES - s.tasks * s.width)))
    return jnp.stack(split_f32(wide) + split_f32(wide.T))


def matern(left, right):
    squared = lax.dot_general(left, right, NT, preferred_element_type=jnp.float32)
    squared = jnp.maximum(squared, 1e-30)
    root = squared * lax.rsqrt(squared)
    decay = jnp.exp2(root * (-math.sqrt(5.0) / math.log(2.0)))
    shaped = ((squared + 0.6) + root * (3.0 / math.sqrt(5.0))) * decay
    return shaped.astype(jnp.bfloat16)


def dot(left, right, dims=None):
    dims = dims or (((1,), (0,)), ((), ()))
    return lax.dot_general(left, right, dims, preferred_element_type=jnp.float32)


def kernel(
    s, low, n_strip, high,
    x_ref, mats_ref, factors_ref, noise_ref, out_ref,
    rows, cols, col_w, col_r, row_r, row_sums, col_sums,
    row_out, row_in, col_out, col_in,
    row_send, row_recv, col_send, col_recv, back_send, back_recv, side_send, side_recv,
):
    n = x_ref.shape[0]
    n_a, n_b = low * n_strip, high
    half_a, half_b = n_a // 2, n_b // 2
    blk, strip = lax.axis_index("blk"), lax.axis_index("strip")
    mine_b, mine_a = blk // low, (blk % low) * n_strip + strip

    def peer_a(index):
        return (mine_b * low + index // n_strip, index % n_strip)

    def peer_b(index):
        return (index * low + blk % low, strip)

    def copy(src, dst, send, recv, peer):
        return pltpu.make_async_remote_copy(
            src_ref=src, dst_ref=dst, send_sem=send, recv_sem=recv,
            device_id=peer, device_id_type=MESH,
        )

    def row_copy(k):
        return copy(
            x_ref, rows.at[k], row_send.at[k], row_recv.at[k], peer_a((mine_a + k) % n_a)
        )

    def col_copy(k):
        return copy(
            x_ref, cols.at[k], col_send.at[k], col_recv.at[k], peer_b((mine_b + k) % n_b)
        )

    def row_back(k):
        return copy(
            row_out.at[k], row_in.at[k], back_send.at[k], back_recv.at[k],
            peer_a((mine_a + n_a - k) % n_a),
        )

    def col_back(k):
        return copy(
            col_out.at[k], col_in.at[k], side_send.at[k], side_recv.at[k],
            peer_b((mine_b + n_b - k) % n_b),
        )

    barrier = pltpu.get_barrier_semaphore()
    for k in range(1, n_a):
        pl.semaphore_signal(
            barrier, inc=1, device_id=peer_a((mine_a + k) % n_a), device_id_type=MESH
        )
    for k in range(1, n_b):
        pl.semaphore_signal(
            barrier, inc=1, device_id=peer_b((mine_b + k) % n_b), device_id_type=MESH
        )
    rows[0] = x_ref[...]
    cols[0] = x_ref[...]
    row_sums[...] = jnp.zeros_like(row_sums)
    col_sums[...] = jnp.zeros_like(col_sums)
    pl.semaphore_wait(barrier, n_a + n_b - 2)

    for k in range(1, half_a + 1):
        row_copy(k).start()
    for gi in range(1, n_b):
        col_copy((gi + 1) // 2 if gi % 2 else n_b - gi // 2).start()

    def group(gi, _):
        kb = jnp.where(gi % 2 == 1, (gi + 1) // 2, (n_b - gi // 2) % n_b)

        @pl.when(gi > 0)
        def _():
            col_copy(kb).wait_recv()

        block = cols[kb]
        col_w[...] = dot(block, mats_ref[0]).astype(jnp.bfloat16)
        col_r[...] = (dot(block, mats_ref[1]) * dot(block, mats_ref[2])).astype(jnp.bfloat16)

        def tile(t, _):
            ka = jnp.where(gi == 0, t, (t + 1) % (half_a + 1))

            @pl.when(gi == 0)
            def _():
                @pl.when(t > 0)
                def _():
                    row_copy(ka).wait_recv()

                block = rows[ka]
                row_r[ka] = (
                    dot(mats_ref[3], block, NT) * dot(mats_ref[4], block, NT)
                ).astype(jnp.bfloat16)

            alone = jnp.logical_and(
                jnp.logical_or(ka == 0, ka == half_a), jnp.logical_or(kb == 0, kb == half_b)
            )
            side = jnp.where(alone, n_b, kb)
            shaped = matern(rows[ka], col_w[...])
            row_sums[ka] = row_sums[ka] + dot(shaped, col_r[...])
            col_sums[side] = col_sums[side] + dot(row_r[ka], shaped)

            @pl.when(gi == n_b - 1)
            def _():
                block = rows[ka]
                factor = dot(block, factors_ref[0])
                for piece in range(1, PIECES):
                    factor = factor + dot(block, factors_ref[piece])
                total = row_sums[ka] * factor
                turn = s.width
                while turn < LANES:
                    total = total + pltpu.roll(total, turn, 1)
                    turn *= 2
                part = n // s.tasks
                lane = lax.broadcasted_iota(jnp.int32, (part, LANES), 1)
                packed = total[:part]
                for i in range(1, s.tasks):
                    packed = jnp.where(lane >= i * s.width, total[i * part:(i + 1) * part], packed)
                row_out[ka] = packed

                @pl.when(ka > 0)
                def _():
                    row_back(ka).start()

            return 0

        lax.fori_loop(0, jnp.where(kb <= half_b, half_a + 1, half_a - 1), tile, 0)
        block = cols[kb]
        factor = dot(factors_ref[PIECES], block, NT)
        for piece in range(1, PIECES):
            factor = factor + dot(factors_ref[PIECES + piece], block, NT)
        total = col_sums[kb] * factor
        packed = total[:s.width]
        for i in range(1, s.tasks):
            packed = packed + total[i * s.width:(i + 1) * s.width]
        col_out[kb] = packed

        @pl.when(gi > 0)
        def _():
            col_back(kb).start()

        return 0

    lax.fori_loop(0, n_b, group, 0)
    side = col_out[0]
    for k in range(1, n_b):
        col_back(k).wait_recv()
        side = side + col_in[k]
    side = side.T
    total = row_out[0]
    for k in range(1, half_a + 1):
        row_back(k).wait_recv()
        total = total + row_in[k]
    part = n // s.tasks
    for i in range(s.tasks):
        span = slice(i * part, (i + 1) * part)
        out_ref[span, :] = (
            total[:, i * s.width:(i + 1) * s.width]
            + side[span]
            + noise_ref[0] * x_ref[span, s.rhs:].astype(jnp.float32)
        )
    for k in range(1, half_a + 1):
        row_copy(k).wait_send()
        row_back(k).wait_send()
    for k in range(1, n_b):
        col_copy(k).wait_send()
        col_back(k).wait_send()


def solution(mesh):
    n_blk, n_strip = mesh.shape["blk"], mesh.shape["strip"]
    low = low_size(n_blk, n_strip)
    high = n_blk // low
    n_a, n_b = low * n_strip, high
    assert n_a % 2 == 0 and n_b % 2 == 0
    half = n_a // 2 + 1

    def body(points, task_ids, rhs, length_scales, coregion, noise):
        n = points.shape[0]
        s = Sizes(points.shape[1], coregion.shape[0], rhs.shape[1])
        packed = pack_points(points, task_ids, rhs, length_scales, s)
        vmem = pl.BlockSpec(memory_space=pltpu.VMEM)
        bf16, f32 = jnp.bfloat16, jnp.float32
        return pl.pallas_call(
            functools.partial(kernel, s, low, n_strip, high),
            out_shape=jax.ShapeDtypeStruct((n, s.width), f32),
            in_specs=[vmem, vmem, vmem, pl.BlockSpec(memory_space=pltpu.SMEM)],
            out_specs=vmem,
            scratch_shapes=[
                pltpu.VMEM((half, n, LANES), bf16),
                pltpu.VMEM((n_b, n, LANES), bf16),
                pltpu.VMEM((n, LANES), bf16),
                pltpu.VMEM((n, LANES), bf16),
                pltpu.VMEM((half, LANES, n), bf16),
                pltpu.VMEM((half, n, LANES), f32),
                pltpu.VMEM((n_b + 1, LANES, n), f32),
                pltpu.VMEM((half, n // s.tasks, LANES), f32),
                pltpu.VMEM((half, n // s.tasks, LANES), f32),
                pltpu.VMEM((n_b, s.width, n), f32),
                pltpu.VMEM((n_b, s.width, n), f32),
                *[pltpu.SemaphoreType.DMA((half,))] * 2,
                *[pltpu.SemaphoreType.DMA((n_b,))] * 2,
                *[pltpu.SemaphoreType.DMA((half,))] * 2,
                *[pltpu.SemaphoreType.DMA((n_b,))] * 2,
            ],
            compiler_params=pltpu.CompilerParams(
                collective_id=0, has_side_effects=True, vmem_limit_bytes=60000 * 1024
            ),
        )(packed, constant_mats(s), factor_mats(coregion, s), noise)

    return jax.shard_map(
        body,
        mesh=mesh,
        in_specs=(
            P(("blk", "strip"), None),
            P(("blk", "strip")),
            P(("blk", "strip"), None),
            P(),
            P(),
            P(),
        ),
        out_specs=P(("blk", "strip"), None),
        check_vma=False,
    )
```

```python
import functools
import math

import jax
import jax.numpy as jnp
from jax import lax
from jax.experimental import pallas as pl
from jax.experimental.pallas import tpu as pltpu
from jax.sharding import PartitionSpec as P

MESH = pl.DeviceIdType.MESH
LANES = 128
NT = (((1,), (1,)), ((), ()))
PIECES = 3


def low_size(n_blk, n_strip):
    for size in range(1, n_blk + 1):
        if n_blk % size == 0 and size * n_strip >= n_blk // size:
            return size
    return n_blk


class Sizes:
    def __init__(self, feat, tasks, width):
        self.feat, self.tasks, self.width = feat, tasks, width
        self.norm = feat
        self.one = feat + PIECES
        self.hot = feat + 2 * PIECES
        self.rhs = LANES - width


def build_mats(s, coregion_ref, mats, factors):
    for flip in (0, 1):
        own = lax.broadcasted_iota(jnp.int32, (LANES, LANES), flip)
        wide = lax.broadcasted_iota(jnp.int32, (LANES, LANES), 1 - flip)
        zero = jnp.zeros((LANES, LANES), jnp.float32)
        hots, vals, factor = zero, zero, zero
        for t in range(s.tasks):
            inside = jnp.logical_and(wide >= t * s.width, wide < (t + 1) * s.width)
            hots = jnp.where(jnp.logical_and(inside, own == s.hot + t), 1.0, hots)
            vals = jnp.where(jnp.logical_and(inside, own == wide + (s.rhs - t * s.width)), 1.0, vals)
            for b in range(s.tasks):
                factor = jnp.where(
                    jnp.logical_and(inside, own == s.hot + b),
                    coregion_ref[b, t] * jnp.float32(5.0 / 3.0),
                    factor,
                )
        mats[1 + 2 * flip] = hots.astype(jnp.bfloat16)
        mats[2 + 2 * flip] = vals.astype(jnp.bfloat16)
        for piece in range(PIECES):
            top = factor.astype(jnp.bfloat16)
            factors[flip * PIECES + piece] = top
            factor = factor - top.astype(jnp.float32)
        if not flip:
            swap = jnp.where(jnp.logical_and(own == wide, own < s.feat), -2.0, zero)
            for i in range(PIECES):
                there = jnp.logical_and(own == s.one + i, wide == s.norm + i)
                back = jnp.logical_and(own == s.norm + i, wide == s.one + i)
                swap = jnp.where(jnp.logical_or(there, back), 1.0, swap)
            mats[0] = swap.astype(jnp.bfloat16)


def pack_points(s, points_ref, ids_ref, rhs_ref, scales_ref):
    n = points_ref.shape[1]
    scales = jnp.broadcast_to(scales_ref[...], (8, s.feat)).T[:, :1]
    scaled = (points_ref[...].astype(jnp.float32) / scales).astype(jnp.bfloat16)
    scaled = scaled.astype(jnp.float32)
    rest = jnp.sum(scaled * scaled, axis=0, keepdims=True)
    height = s.rhs - s.feat
    row = lax.broadcasted_iota(jnp.int32, (height, n), 0) + s.feat
    extra = jnp.where(jnp.logical_and(row >= s.one, row < s.one + PIECES), 1.0, 0.0)
    for i in range(PIECES):
        top = rest.astype(jnp.bfloat16).astype(jnp.float32)
        extra = jnp.where(row == s.norm + i, top, extra)
        rest = rest - top
    extra = jnp.where(row - s.hot == ids_ref[...], 1.0, extra)
    packed = jnp.concatenate([scaled, extra, rhs_ref[...].astype(jnp.float32)], axis=0)
    return packed.T.astype(jnp.bfloat16)


def matern(left, right):
    squared = lax.dot_general(left, right, NT, preferred_element_type=jnp.float32)
    squared = jnp.maximum(squared, 1e-30)
    root = squared * lax.rsqrt(squared)
    decay = jnp.exp2(root * (-math.sqrt(5.0) / math.log(2.0)))
    shaped = ((squared + 0.6) + root * (3.0 / math.sqrt(5.0))) * decay
    return shaped.astype(jnp.bfloat16)


def dot(left, right, dims=None):
    dims = dims or (((1,), (0,)), ((), ()))
    return lax.dot_general(left, right, dims, preferred_element_type=jnp.float32)


def kernel(
    s, low, n_strip, high,
    points_ref, ids_ref, rhs_ref, scales_ref, coregion_ref, noise_ref, out_ref,
    mats_ref, factors_ref, rows, cols, col_w, col_r, row_r, row_sums, col_sums,
    row_out, row_in, col_out, col_in, flat,
    row_send, row_recv, col_send, col_recv, back_send, back_recv, side_send, side_recv,
):
    n = points_ref.shape[1]
    n_a, n_b = low * n_strip, high
    half_a, half_b = n_a // 2, n_b // 2
    blk, strip = lax.axis_index("blk"), lax.axis_index("strip")
    mine_b, mine_a = blk // low, (blk % low) * n_strip + strip

    def peer_a(index):
        return (mine_b * low + index // n_strip, index % n_strip)

    def peer_b(index):
        return (index * low + blk % low, strip)

    def copy(src, dst, send, recv, peer):
        return pltpu.make_async_remote_copy(
            src_ref=src, dst_ref=dst, send_sem=send, recv_sem=recv,
            device_id=peer, device_id_type=MESH,
        )

    def row_copy(k):
        return copy(
            rows.at[0], rows.at[k], row_send.at[k], row_recv.at[k], peer_a((mine_a + k) % n_a)
        )

    def col_copy(k):
        return copy(
            rows.at[0], cols.at[k], col_send.at[k], col_recv.at[k], peer_b((mine_b + k) % n_b)
        )

    def row_back(k):
        return copy(
            row_out.at[k], row_in.at[k], back_send.at[k], back_recv.at[k],
            peer_a((mine_a + n_a - k) % n_a),
        )

    def col_back(k):
        return copy(
            col_out.at[k], col_in.at[k], side_send.at[k], side_recv.at[k],
            peer_b((mine_b + n_b - k) % n_b),
        )

    barrier = pltpu.get_barrier_semaphore()
    for k in range(1, n_a):
        pl.semaphore_signal(
            barrier, inc=1, device_id=peer_a((mine_a + k) % n_a), device_id_type=MESH
        )
    for k in range(1, n_b):
        pl.semaphore_signal(
            barrier, inc=1, device_id=peer_b((mine_b + k) % n_b), device_id_type=MESH
        )
    mine = pack_points(s, points_ref, ids_ref, rhs_ref, scales_ref)
    rows[0] = mine
    cols[0] = mine
    build_mats(s, coregion_ref, mats_ref, factors_ref)
    pl.semaphore_wait(barrier, n_a + n_b - 2)

    for k in range(1, half_a + 1):
        row_copy(k).start()
    for gi in range(1, n_b):
        col_copy((gi + 1) // 2 if gi % 2 else n_b - gi // 2).start()

    row_sums[...] = jnp.zeros_like(row_sums)
    col_sums[...] = jnp.zeros_like(col_sums)

    def group(gi, _):
        kb = jnp.where(gi % 2 == 1, (gi + 1) // 2, (n_b - gi // 2) % n_b)

        @pl.when(gi > 0)
        def _():
            col_copy(kb).wait_recv()

        block = cols[kb]
        col_w[...] = dot(block, mats_ref[0]).astype(jnp.bfloat16)
        col_r[...] = (dot(block, mats_ref[1]) * dot(block, mats_ref[2])).astype(jnp.bfloat16)

        def tile(t, _):
            ka = jnp.where(gi == 0, t, (t + 1) % (half_a + 1))

            @pl.when(gi == 0)
            def _():
                @pl.when(t > 0)
                def _():
                    row_copy(ka).wait_recv()

                block = rows[ka]
                row_r[ka] = (
                    dot(mats_ref[3], block, NT) * dot(mats_ref[4], block, NT)
                ).astype(jnp.bfloat16)

            alone = jnp.logical_and(
                jnp.logical_or(ka == 0, ka == half_a), jnp.logical_or(kb == 0, kb == half_b)
            )
            side = jnp.where(alone, n_b, kb)
            shaped = matern(rows[ka], col_w[...])
            row_sums[ka] = row_sums[ka] + dot(shaped, col_r[...])
            col_sums[side] = col_sums[side] + dot(row_r[ka], shaped)

            @pl.when(gi == n_b - 1)
            def _():
                block = rows[ka]
                factor = dot(block, factors_ref[0])
                for piece in range(1, PIECES):
                    factor = factor + dot(block, factors_ref[piece])
                total = row_sums[ka] * factor
                turn = s.width
                while turn < LANES:
                    total = total + pltpu.roll(total, turn, 1)
                    turn *= 2
                part = n // s.tasks
                lane = lax.broadcasted_iota(jnp.int32, (part, LANES), 1)
                packed = total[:part]
                for i in range(1, s.tasks):
                    packed = jnp.where(lane >= i * s.width, total[i * part:(i + 1) * part], packed)
                row_out[ka] = packed

                @pl.when(ka > 0)
                def _():
                    row_back(ka).start()

            return 0

        lax.fori_loop(0, jnp.where(kb <= half_b, half_a + 1, half_a - 1), tile, 0)
        block = cols[kb]
        factor = dot(factors_ref[PIECES], block, NT)
        for piece in range(1, PIECES):
            factor = factor + dot(factors_ref[PIECES + piece], block, NT)
        total = col_sums[kb] * factor
        packed = total[:s.width]
        for i in range(1, s.tasks):
            packed = packed + total[i * s.width:(i + 1) * s.width]
        col_out[kb] = packed

        @pl.when(gi > 0)
        def _():
            col_back(kb).start()

        return 0

    lax.fori_loop(0, n_b, group, 0)
    side = col_out[0]
    for k in range(1, n_b):
        col_back(k).wait_recv()
        side = side + col_in[k]
    total = row_out[0]
    for k in range(1, half_a + 1):
        row_back(k).wait_recv()
        total = total + row_in[k]
    part = n // s.tasks
    for i in range(s.tasks):
        flat[i * part:(i + 1) * part, :] = total[:, i * s.width:(i + 1) * s.width]
    out_ref[...] = side + flat[...].T + noise_ref[0] * rhs_ref[...].astype(jnp.float32)
    for k in range(1, half_a + 1):
        row_copy(k).wait_send()
        row_back(k).wait_send()
    for k in range(1, n_b):
        col_copy(k).wait_send()
        col_back(k).wait_send()


def solution(mesh):
    n_blk, n_strip = mesh.shape["blk"], mesh.shape["strip"]
    low = low_size(n_blk, n_strip)
    high = n_blk // low
    n_a, n_b = low * n_strip, high
    assert n_a % 2 == 0 and n_b % 2 == 0
    half = n_a // 2 + 1

    def body(points, task_ids, rhs, length_scales, coregion, noise):
        n = points.shape[0]
        s = Sizes(points.shape[1], coregion.shape[0], rhs.shape[1])
        vmem = pl.BlockSpec(memory_space=pltpu.VMEM)
        smem = pl.BlockSpec(memory_space=pltpu.SMEM)
        bf16, f32 = jnp.bfloat16, jnp.float32
        return pl.pallas_call(
            functools.partial(kernel, s, low, n_strip, high),
            out_shape=jax.ShapeDtypeStruct((s.width, n), f32),
            in_specs=[vmem, vmem, vmem, vmem, smem, smem],
            out_specs=vmem,
            scratch_shapes=[
                pltpu.VMEM((5, LANES, LANES), bf16),
                pltpu.VMEM((2 * PIECES, LANES, LANES), bf16),
                pltpu.VMEM((half, n, LANES), bf16),
                pltpu.VMEM((n_b, n, LANES), bf16),
                pltpu.VMEM((n, LANES), bf16),
                pltpu.VMEM((n, LANES), bf16),
                pltpu.VMEM((half, LANES, n), bf16),
                pltpu.VMEM((half, n, LANES), f32),
                pltpu.VMEM((n_b + 1, LANES, n), f32),
                pltpu.VMEM((half, n // s.tasks, LANES), f32),
                pltpu.VMEM((half, n // s.tasks, LANES), f32),
                pltpu.VMEM((n_b, s.width, n), f32),
                pltpu.VMEM((n_b, s.width, n), f32),
                pltpu.VMEM((n, s.width), f32),
                *[pltpu.SemaphoreType.DMA((half,))] * 2,
                *[pltpu.SemaphoreType.DMA((n_b,))] * 2,
                *[pltpu.SemaphoreType.DMA((half,))] * 2,
                *[pltpu.SemaphoreType.DMA((n_b,))] * 2,
            ],
            compiler_params=pltpu.CompilerParams(
                collective_id=0, has_side_effects=True, vmem_limit_bytes=60000 * 1024
            ),
        )(points.T, task_ids[None, :], rhs.T, length_scales[None, :], coregion, noise).T

    return jax.shard_map(
        body,
        mesh=mesh,
        in_specs=(
            P(("blk", "strip"), None),
            P(("blk", "strip")),
            P(("blk", "strip"), None),
            P(),
            P(),
            P(),
        ),
        out_specs=P(("blk", "strip"), None),
        check_vma=False,
    )
```

```python
import functools
import math

import jax
import jax.numpy as jnp
from jax import lax
from jax.experimental import pallas as pl
from jax.experimental.pallas import tpu as pltpu
from jax.sharding import PartitionSpec as P

MESH = pl.DeviceIdType.MESH
LANES = 128
NT = (((1,), (1,)), ((), ()))
PIECES = 3


def low_size(n_blk, n_strip):
    for size in range(1, n_blk + 1):
        if n_blk % size == 0 and size * n_strip >= n_blk // size:
            return size
    return n_blk


class Sizes:
    def __init__(self, feat, tasks, width):
        self.feat, self.tasks, self.width = feat, tasks, width
        self.norm = feat
        self.one = feat + PIECES
        self.hot = feat + 2 * PIECES
        self.rhs = LANES - width


def build_mats(s, coregion_ref, mats, factors_ref):
    for flip in (0, 1):
        own = lax.broadcasted_iota(jnp.int32, (LANES, LANES), flip)
        wide = lax.broadcasted_iota(jnp.int32, (LANES, LANES), 1 - flip)
        zero = jnp.zeros((LANES, LANES), jnp.float32)
        hots, vals, factors = zero, zero, zero
        for t in range(s.tasks):
            inside = jnp.logical_and(wide >= t * s.width, wide < (t + 1) * s.width)
            hots = jnp.where(jnp.logical_and(inside, own == s.hot + t), 1.0, hots)
            vals = jnp.where(jnp.logical_and(inside, own == wide + (s.rhs - t * s.width)), 1.0, vals)
            for b in range(s.tasks):
                rest = jnp.full((LANES, LANES), coregion_ref[b, t] * jnp.float32(5.0 / 3.0))
                for piece in range(PIECES):
                    top = rest.astype(jnp.bfloat16).astype(jnp.float32)
                    here = own == s.hot + piece * s.tasks + b
                    factors = jnp.where(jnp.logical_and(inside, here), top, factors)
                    rest = rest - top
        mats[1 + 2 * flip] = hots.astype(jnp.bfloat16)
        mats[2 + 2 * flip] = vals.astype(jnp.bfloat16)
        if flip:
            folds = zero
            for t in range(s.tasks):
                folds = jnp.where(own == wide + t * s.width, 1.0, folds)
            mats[5] = folds.astype(jnp.bfloat16)
        factors_ref[flip] = factors.astype(jnp.bfloat16)
        if not flip:
            swap = jnp.where(jnp.logical_and(own == wide, own < s.feat), -2.0, zero)
            for i in range(PIECES):
                there = jnp.logical_and(own == s.one + i, wide == s.norm + i)
                back = jnp.logical_and(own == s.norm + i, wide == s.one + i)
                swap = jnp.where(jnp.logical_or(there, back), 1.0, swap)
            mats[0] = swap.astype(jnp.bfloat16)


def pack_points(s, points_ref, ids_ref, rhs_ref, scales_ref):
    n = points_ref.shape[1]
    scales = jnp.broadcast_to(scales_ref[...], (8, s.feat)).T[:, :1]
    scaled = (points_ref[...].astype(jnp.float32) / scales).astype(jnp.bfloat16)
    scaled = scaled.astype(jnp.float32)
    rest = jnp.sum(scaled * scaled, axis=0, keepdims=True)
    height = s.rhs - s.feat
    row = lax.broadcasted_iota(jnp.int32, (height, n), 0) + s.feat
    extra = jnp.where(jnp.logical_and(row >= s.one, row < s.one + PIECES), 1.0, 0.0)
    for i in range(PIECES):
        top = rest.astype(jnp.bfloat16).astype(jnp.float32)
        extra = jnp.where(row == s.norm + i, top, extra)
        rest = rest - top
    for i in range(PIECES):
        extra = jnp.where(row - (s.hot + i * s.tasks) == ids_ref[...], 1.0, extra)
    packed = jnp.concatenate([scaled, extra, rhs_ref[...].astype(jnp.float32)], axis=0)
    return packed.T.astype(jnp.bfloat16)


def matern(squared):
    squared = jnp.maximum(squared, 1e-30)
    root = squared * lax.rsqrt(squared)
    decay = jnp.exp2(root * (-math.sqrt(5.0) / math.log(2.0)))
    shaped = ((squared + 0.6) + root * (3.0 / math.sqrt(5.0))) * decay
    return shaped.astype(jnp.bfloat16)


def dot(left, right, dims=None):
    dims = dims or (((1,), (0,)), ((), ()))
    return lax.dot_general(left, right, dims, preferred_element_type=jnp.float32)


def kernel(
    s, low, n_strip, high,
    points_ref, ids_ref, rhs_ref, scales_ref, coregion_ref, noise_ref, out_ref,
    mats_ref, factors_ref, rows, cols, col_w, col_r, row_r, row_sums, col_sums,
    row_out, row_in, col_out, col_in,
    row_send, row_recv, col_send, col_recv, back_send, back_recv, side_send, side_recv,
):
    n = points_ref.shape[1]
    n_a, n_b = low * n_strip, high
    half_a, half_b = n_a // 2, n_b // 2
    blk, strip = lax.axis_index("blk"), lax.axis_index("strip")
    mine_b, mine_a = blk // low, (blk % low) * n_strip + strip

    def peer_a(index):
        return (mine_b * low + index // n_strip, index % n_strip)

    def peer_b(index):
        return (index * low + blk % low, strip)

    def copy(src, dst, send, recv, peer):
        return pltpu.make_async_remote_copy(
            src_ref=src, dst_ref=dst, send_sem=send, recv_sem=recv,
            device_id=peer, device_id_type=MESH,
        )

    def row_copy(k):
        return copy(
            rows.at[0], rows.at[k], row_send.at[k], row_recv.at[k], peer_a((mine_a + k) % n_a)
        )

    def col_copy(k):
        return copy(
            rows.at[0], cols.at[k], col_send.at[k], col_recv.at[k], peer_b((mine_b + k) % n_b)
        )

    def row_back(k):
        return copy(
            row_out.at[k], row_in.at[k], back_send.at[k], back_recv.at[k],
            peer_a((mine_a + n_a - k) % n_a),
        )

    def col_back(k):
        return copy(
            col_out.at[k], col_in.at[k], side_send.at[k], side_recv.at[k],
            peer_b((mine_b + n_b - k) % n_b),
        )

    barrier = pltpu.get_barrier_semaphore()
    for k in range(1, n_a):
        pl.semaphore_signal(
            barrier, inc=1, device_id=peer_a((mine_a + k) % n_a), device_id_type=MESH
        )
    for k in range(1, n_b):
        pl.semaphore_signal(
            barrier, inc=1, device_id=peer_b((mine_b + k) % n_b), device_id_type=MESH
        )
    mine = pack_points(s, points_ref, ids_ref, rhs_ref, scales_ref)
    rows[0] = mine
    cols[0] = mine
    build_mats(s, coregion_ref, mats_ref, factors_ref)
    row_sums[...] = jnp.zeros_like(row_sums)
    col_sums[...] = jnp.zeros_like(col_sums)
    pl.semaphore_wait(barrier, n_a + n_b - 2)

    for k in range(1, half_a + 1):
        row_copy(k).start()
    for gi in range(1, n_b):
        col_copy((gi + 1) // 2 if gi % 2 else n_b - gi // 2).start()


    def group(gi, _):
        kb = jnp.where(gi % 2 == 1, (gi + 1) // 2, (n_b - gi // 2) % n_b)

        @pl.when(gi > 0)
        def _():
            col_copy(kb).wait_recv()

        block = cols[kb]
        col_w[...] = dot(block, mats_ref[0]).astype(jnp.bfloat16)
        col_r[...] = (dot(block, mats_ref[1]) * dot(block, mats_ref[2])).astype(jnp.bfloat16)

        def tile(t, _):
            ka = jnp.where(gi == 0, t, (t + 1) % (half_a + 1))

            @pl.when(gi == 0)
            def _():
                @pl.when(t > 0)
                def _():
                    row_copy(ka).wait_recv()

                block = rows[ka]
                row_r[ka] = (
                    dot(mats_ref[3], block, NT) * dot(mats_ref[4], block, NT)
                ).astype(jnp.bfloat16)

            alone = jnp.logical_and(
                jnp.logical_or(ka == 0, ka == half_a), jnp.logical_or(kb == 0, kb == half_b)
            )
            side = jnp.where(alone, n_b, kb)
            shaped = matern(dot(rows[ka], col_w[...], NT))
            row_sums[ka] = row_sums[ka] + dot(shaped, col_r[...])
            col_sums[side] = col_sums[side] + dot(row_r[ka], shaped)

            @pl.when(gi == n_b - 1)
            def _():
                rest = row_sums[ka] * dot(rows[ka], factors_ref[0])
                packed = jnp.zeros((s.width, n), jnp.float32)
                for _ in range(PIECES):
                    top = rest.astype(jnp.bfloat16)
                    packed = packed + dot(mats_ref[5, :s.width, :], top, NT)
                    rest = rest - top.astype(jnp.float32)
                row_out[ka] = packed

                @pl.when(ka > 0)
                def _():
                    row_back(ka).start()

            return 0

        lax.fori_loop(0, jnp.where(kb <= half_b, half_a + 1, half_a - 1), tile, 0)
        total = col_sums[kb] * dot(factors_ref[1], cols[kb], NT)
        packed = total[:s.width]
        for i in range(1, s.tasks):
            packed = packed + total[i * s.width:(i + 1) * s.width]
        col_out[kb] = packed

        @pl.when(gi > 0)
        def _():
            col_back(kb).start()

        return 0

    lax.fori_loop(0, n_b, group, 0)
    side = col_out[0]
    for k in range(1, n_b):
        col_back(k).wait_recv()
        side = side + col_in[k]
    side = side + row_out[0]
    for k in range(1, half_a + 1):
        row_back(k).wait_recv()
        side = side + row_in[k]
    out_ref[...] = side + noise_ref[0] * rhs_ref[...].astype(jnp.float32)
    for k in range(1, half_a + 1):
        row_copy(k).wait_send()
        row_back(k).wait_send()
    for k in range(1, n_b):
        col_copy(k).wait_send()
        col_back(k).wait_send()


def solution(mesh):
    n_blk, n_strip = mesh.shape["blk"], mesh.shape["strip"]
    low = low_size(n_blk, n_strip)
    high = n_blk // low
    n_a, n_b = low * n_strip, high
    assert n_a % 2 == 0 and n_b % 2 == 0
    half = n_a // 2 + 1

    def body(points, task_ids, rhs, length_scales, coregion, noise):
        n = points.shape[0]
        s = Sizes(points.shape[1], coregion.shape[0], rhs.shape[1])
        vmem = pl.BlockSpec(memory_space=pltpu.VMEM)
        smem = pl.BlockSpec(memory_space=pltpu.SMEM)
        bf16, f32 = jnp.bfloat16, jnp.float32
        return pl.pallas_call(
            functools.partial(kernel, s, low, n_strip, high),
            out_shape=jax.ShapeDtypeStruct((s.width, n), f32),
            in_specs=[vmem, vmem, vmem, vmem, smem, smem],
            out_specs=vmem,
            scratch_shapes=[
                pltpu.VMEM((6, LANES, LANES), bf16),
                pltpu.VMEM((2, LANES, LANES), bf16),
                pltpu.VMEM((half, n, LANES), bf16),
                pltpu.VMEM((n_b, n, LANES), bf16),
                pltpu.VMEM((n, LANES), bf16),
                pltpu.VMEM((n, LANES), bf16),
                pltpu.VMEM((half, LANES, n), bf16),
                pltpu.VMEM((half, n, LANES), f32),
                pltpu.VMEM((n_b + 1, LANES, n), f32),
                pltpu.VMEM((half, s.width, n), f32),
                pltpu.VMEM((half, s.width, n), f32),
                pltpu.VMEM((n_b, s.width, n), f32),
                pltpu.VMEM((n_b, s.width, n), f32),
                *[pltpu.SemaphoreType.DMA((half,))] * 2,
                *[pltpu.SemaphoreType.DMA((n_b,))] * 2,
                *[pltpu.SemaphoreType.DMA((half,))] * 2,
                *[pltpu.SemaphoreType.DMA((n_b,))] * 2,
            ],
            compiler_params=pltpu.CompilerParams(
                collective_id=0, has_side_effects=True, vmem_limit_bytes=60000 * 1024
            ),
        )(points.T, task_ids[None, :], rhs.T, length_scales[None, :], coregion, noise).T

    return jax.shard_map(
        body,
        mesh=mesh,
        in_specs=(
            P(("blk", "strip"), None),
            P(("blk", "strip")),
            P(("blk", "strip"), None),
            P(),
            P(),
            P(),
        ),
        out_specs=P(("blk", "strip"), None),
        check_vma=False,
    )
```

```python
import functools
import math

import jax
import jax.numpy as jnp
from jax import lax
from jax.experimental import pallas as pl
from jax.experimental.pallas import tpu as pltpu
from jax.sharding import PartitionSpec as P

MESH = pl.DeviceIdType.MESH
LANES = 128
NT = (((1,), (1,)), ((), ()))
PIECES = 3


def low_size(n_blk, n_strip):
    for size in range(1, n_blk + 1):
        if n_blk % size == 0 and size * n_strip >= n_blk // size:
            return size
    return n_blk


class Sizes:
    def __init__(self, feat, tasks, width):
        self.feat, self.tasks, self.width = feat, tasks, width
        self.norm = feat
        self.one = feat + PIECES
        self.hot = feat + 2 * PIECES
        self.rhs = LANES - width


def build_mats(s, coregion_ref, mats, factors_ref):
    for flip in (0, 1):
        own = lax.broadcasted_iota(jnp.int32, (LANES, LANES), flip)
        wide = lax.broadcasted_iota(jnp.int32, (LANES, LANES), 1 - flip)
        zero = jnp.zeros((LANES, LANES), jnp.float32)
        hots, vals, factors = zero, zero, zero
        for t in range(s.tasks):
            inside = jnp.logical_and(wide >= t * s.width, wide < (t + 1) * s.width)
            hots = jnp.where(jnp.logical_and(inside, own == s.hot + t), 1.0, hots)
            vals = jnp.where(jnp.logical_and(inside, own == wide + (s.rhs - t * s.width)), 1.0, vals)
            for b in range(s.tasks):
                rest = jnp.full((LANES, LANES), coregion_ref[b, t] * jnp.float32(5.0 / 3.0))
                for piece in range(PIECES):
                    top = rest.astype(jnp.bfloat16).astype(jnp.float32)
                    here = own == s.hot + piece * s.tasks + b
                    factors = jnp.where(jnp.logical_and(inside, here), top, factors)
                    rest = rest - top
        mats[1 + 2 * flip] = hots.astype(jnp.bfloat16)
        mats[2 + 2 * flip] = vals.astype(jnp.bfloat16)
        if flip:
            folds = zero
            for t in range(s.tasks):
                folds = jnp.where(own == wide + t * s.width, 1.0, folds)
            mats[5] = folds.astype(jnp.bfloat16)
        factors_ref[flip] = factors.astype(jnp.bfloat16)
        if not flip:
            swap = jnp.where(jnp.logical_and(own == wide, own < s.feat), -2.0, zero)
            for i in range(PIECES):
                there = jnp.logical_and(own == s.one + i, wide == s.norm + i)
                back = jnp.logical_and(own == s.norm + i, wide == s.one + i)
                swap = jnp.where(jnp.logical_or(there, back), 1.0, swap)
            mats[0] = swap.astype(jnp.bfloat16)


def pack_points(s, points_ref, ids_ref, rhs_ref, scales_ref):
    n = points_ref.shape[1]
    scales = jnp.broadcast_to(scales_ref[...], (8, s.feat)).T[:, :1]
    scaled = (points_ref[...].astype(jnp.float32) / scales).astype(jnp.bfloat16)
    scaled = scaled.astype(jnp.float32)
    rest = jnp.sum(scaled * scaled, axis=0, keepdims=True)
    height = s.rhs - s.feat
    row = lax.broadcasted_iota(jnp.int32, (height, n), 0) + s.feat
    extra = jnp.where(jnp.logical_and(row >= s.one, row < s.one + PIECES), 1.0, 0.0)
    for i in range(PIECES):
        top = rest.astype(jnp.bfloat16).astype(jnp.float32)
        extra = jnp.where(row == s.norm + i, top, extra)
        rest = rest - top
    for i in range(PIECES):
        extra = jnp.where(row - (s.hot + i * s.tasks) == ids_ref[...], 1.0, extra)
    packed = jnp.concatenate([scaled, extra, rhs_ref[...].astype(jnp.float32)], axis=0)
    return packed.T.astype(jnp.bfloat16)


def matern(squared):
    squared = jnp.maximum(squared, 1e-30)
    root = squared * lax.rsqrt(squared)
    decay = jnp.exp2(root * (-math.sqrt(5.0) / math.log(2.0)))
    shaped = ((squared + 0.6) + root * (3.0 / math.sqrt(5.0))) * decay
    return shaped.astype(jnp.bfloat16)


def dot(left, right, dims=None):
    dims = dims or (((1,), (0,)), ((), ()))
    return lax.dot_general(left, right, dims, preferred_element_type=jnp.float32)


def kernel(
    s, low, n_strip, high,
    points_ref, ids_ref, rhs_ref, scales_ref, coregion_ref, noise_ref, out_ref,
    mats_ref, factors_ref, rows, cols, col_w, col_r, row_r, row_sums, col_sums,
    row_out, row_in, col_out, col_in,
    row_send, row_recv, col_send, col_recv, back_send, back_recv, side_send, side_recv,
):
    n = points_ref.shape[1]
    n_a, n_b = low * n_strip, high
    half_a, half_b = n_a // 2, n_b // 2
    blk, strip = lax.axis_index("blk"), lax.axis_index("strip")
    mine_b, mine_a = blk // low, (blk % low) * n_strip + strip

    def peer_a(index):
        return (mine_b * low + index // n_strip, index % n_strip)

    def peer_b(index):
        return (index * low + blk % low, strip)

    def copy(src, dst, send, recv, peer):
        return pltpu.make_async_remote_copy(
            src_ref=src, dst_ref=dst, send_sem=send, recv_sem=recv,
            device_id=peer, device_id_type=MESH,
        )

    def row_copy(k):
        return copy(
            rows.at[0], rows.at[k], row_send.at[k], row_recv.at[k], peer_a((mine_a + k) % n_a)
        )

    def col_copy(k):
        return copy(
            rows.at[0], cols.at[k], col_send.at[k], col_recv.at[k], peer_b((mine_b + k) % n_b)
        )

    def row_back(k):
        return copy(
            row_out.at[k], row_in.at[k], back_send.at[k], back_recv.at[k],
            peer_a((mine_a + n_a - k) % n_a),
        )

    def col_back(k):
        return copy(
            col_out.at[k], col_in.at[k], side_send.at[k], side_recv.at[k],
            peer_b((mine_b + n_b - k) % n_b),
        )

    barrier = pltpu.get_barrier_semaphore()
    for k in range(1, n_a):
        pl.semaphore_signal(
            barrier, inc=1, device_id=peer_a((mine_a + k) % n_a), device_id_type=MESH
        )
    for k in range(1, n_b):
        pl.semaphore_signal(
            barrier, inc=1, device_id=peer_b((mine_b + k) % n_b), device_id_type=MESH
        )
    mine = pack_points(s, points_ref, ids_ref, rhs_ref, scales_ref)
    rows[0] = mine
    cols[0] = mine
    build_mats(s, coregion_ref, mats_ref, factors_ref)
    row_sums[...] = jnp.zeros_like(row_sums)
    col_sums[...] = jnp.zeros_like(col_sums)
    pl.semaphore_wait(barrier, n_a + n_b - 2)

    for k in range(1, half_a + 1):
        row_copy(k).start()
    for gi in range(1, n_b):
        col_copy((gi + 1) // 2 if gi % 2 else n_b - gi // 2).start()


    def send_col(kb):
        total = col_sums[kb] * dot(factors_ref[1], cols[kb], NT)
        packed = total[:s.width]
        for i in range(1, s.tasks):
            packed = packed + total[i * s.width:(i + 1) * s.width]
        col_out[kb] = packed

        @pl.when(kb > 0)
        def _():
            col_back(kb).start()

    def group(gi, _):
        kb = jnp.where(gi % 2 == 1, (gi + 1) // 2, (n_b - gi // 2) % n_b)

        @pl.when(gi > 0)
        def _():
            col_copy(kb).wait_recv()

        block = cols[kb]
        col_w[...] = dot(block, mats_ref[0]).astype(jnp.bfloat16)
        col_r[...] = (dot(block, mats_ref[1]) * dot(block, mats_ref[2])).astype(jnp.bfloat16)

        def tile(t, _):
            ka = jnp.where(gi == 0, t, (t + 1) % (half_a + 1))

            @pl.when(gi == 0)
            def _():
                @pl.when(t > 0)
                def _():
                    row_copy(ka).wait_recv()

                block = rows[ka]
                row_r[ka] = (
                    dot(mats_ref[3], block, NT) * dot(mats_ref[4], block, NT)
                ).astype(jnp.bfloat16)

            alone = jnp.logical_and(
                jnp.logical_or(ka == 0, ka == half_a), jnp.logical_or(kb == 0, kb == half_b)
            )
            side = jnp.where(alone, n_b, kb)
            shaped = matern(dot(rows[ka], col_w[...], NT))
            row_sums[ka] = row_sums[ka] + dot(shaped, col_r[...])
            col_sums[side] = col_sums[side] + dot(row_r[ka], shaped)

            @pl.when(jnp.logical_and(gi == n_b - 1, ka == half_a - 1))
            def _():
                send_col(kb)

            @pl.when(gi == n_b - 1)
            def _():
                rest = row_sums[ka] * dot(rows[ka], factors_ref[0])
                packed = jnp.zeros((s.width, n), jnp.float32)
                for _ in range(PIECES):
                    top = rest.astype(jnp.bfloat16)
                    packed = packed + dot(mats_ref[5, :s.width, :], top, NT)
                    rest = rest - top.astype(jnp.float32)
                row_out[ka] = packed

                @pl.when(ka > 0)
                def _():
                    row_back(ka).start()

            return 0

        lax.fori_loop(0, jnp.where(kb <= half_b, half_a + 1, half_a - 1), tile, 0)
        @pl.when(gi < n_b - 1)
        def _():
            send_col(kb)

        return 0

    lax.fori_loop(0, n_b, group, 0)
    side = col_out[0]
    for k in range(1, n_b):
        col_back(k).wait_recv()
        side = side + col_in[k]
    side = side + row_out[0]
    for k in range(1, half_a + 1):
        row_back(k).wait_recv()
        side = side + row_in[k]
    out_ref[...] = side + noise_ref[0] * rhs_ref[...].astype(jnp.float32)
    for k in range(1, half_a + 1):
        row_copy(k).wait_send()
        row_back(k).wait_send()
    for k in range(1, n_b):
        col_copy(k).wait_send()
        col_back(k).wait_send()


def solution(mesh):
    n_blk, n_strip = mesh.shape["blk"], mesh.shape["strip"]
    low = low_size(n_blk, n_strip)
    high = n_blk // low
    n_a, n_b = low * n_strip, high
    assert n_a % 2 == 0 and n_b % 2 == 0 and n_a > 2
    half = n_a // 2 + 1

    def body(points, task_ids, rhs, length_scales, coregion, noise):
        n = points.shape[0]
        s = Sizes(points.shape[1], coregion.shape[0], rhs.shape[1])
        vmem = pl.BlockSpec(memory_space=pltpu.VMEM)
        smem = pl.BlockSpec(memory_space=pltpu.SMEM)
        bf16, f32 = jnp.bfloat16, jnp.float32
        return pl.pallas_call(
            functools.partial(kernel, s, low, n_strip, high),
            out_shape=jax.ShapeDtypeStruct((s.width, n), f32),
            in_specs=[vmem, vmem, vmem, vmem, smem, smem],
            out_specs=vmem,
            scratch_shapes=[
                pltpu.VMEM((6, LANES, LANES), bf16),
                pltpu.VMEM((2, LANES, LANES), bf16),
                pltpu.VMEM((half, n, LANES), bf16),
                pltpu.VMEM((n_b, n, LANES), bf16),
                pltpu.VMEM((n, LANES), bf16),
                pltpu.VMEM((n, LANES), bf16),
                pltpu.VMEM((half, LANES, n), bf16),
                pltpu.VMEM((half, n, LANES), f32),
                pltpu.VMEM((n_b + 1, LANES, n), f32),
                pltpu.VMEM((half, s.width, n), f32),
                pltpu.VMEM((half, s.width, n), f32),
                pltpu.VMEM((n_b, s.width, n), f32),
                pltpu.VMEM((n_b, s.width, n), f32),
                *[pltpu.SemaphoreType.DMA((half,))] * 2,
                *[pltpu.SemaphoreType.DMA((n_b,))] * 2,
                *[pltpu.SemaphoreType.DMA((half,))] * 2,
                *[pltpu.SemaphoreType.DMA((n_b,))] * 2,
            ],
            compiler_params=pltpu.CompilerParams(
                collective_id=0, has_side_effects=True, vmem_limit_bytes=60000 * 1024
            ),
        )(points.T, task_ids[None, :], rhs.T, length_scales[None, :], coregion, noise).T

    return jax.shard_map(
        body,
        mesh=mesh,
        in_specs=(
            P(("blk", "strip"), None),
            P(("blk", "strip")),
            P(("blk", "strip"), None),
            P(),
            P(),
            P(),
        ),
        out_specs=P(("blk", "strip"), None),
        check_vma=False,
    )
```

```python
import functools
import math

import jax
import jax.numpy as jnp
from jax import lax
from jax.experimental import pallas as pl
from jax.experimental.pallas import tpu as pltpu
from jax.sharding import PartitionSpec as P

MESH = pl.DeviceIdType.MESH
LANES = 128
NT = (((1,), (1,)), ((), ()))
PIECES = 3


def low_size(n_blk, n_strip):
    for size in range(1, n_blk + 1):
        if n_blk % size == 0 and size * n_strip >= n_blk // size:
            return size
    return n_blk


class Sizes:
    def __init__(self, feat, tasks, width):
        self.feat, self.tasks, self.width = feat, tasks, width
        self.norm = feat
        self.one = feat + PIECES
        self.hot = feat + 2 * PIECES
        self.rhs = LANES - width


def build_mats(s, coregion_ref, mats, factors_ref):
    for flip in (0, 1):
        own = lax.broadcasted_iota(jnp.int32, (LANES, LANES), flip)
        wide = lax.broadcasted_iota(jnp.int32, (LANES, LANES), 1 - flip)
        zero = jnp.zeros((LANES, LANES), jnp.float32)
        hots, vals, factors = zero, zero, zero
        for t in range(s.tasks):
            inside = jnp.logical_and(wide >= t * s.width, wide < (t + 1) * s.width)
            hots = jnp.where(jnp.logical_and(inside, own == s.hot + t), 1.0, hots)
            vals = jnp.where(jnp.logical_and(inside, own == wide + (s.rhs - t * s.width)), 1.0, vals)
            for b in range(s.tasks):
                rest = jnp.full((LANES, LANES), coregion_ref[b, t] * jnp.float32(5.0 / 3.0))
                for piece in range(PIECES):
                    top = rest.astype(jnp.bfloat16).astype(jnp.float32)
                    here = own == s.hot + piece * s.tasks + b
                    factors = jnp.where(jnp.logical_and(inside, here), top, factors)
                    rest = rest - top
        mats[1 + 2 * flip] = hots.astype(jnp.bfloat16)
        mats[2 + 2 * flip] = vals.astype(jnp.bfloat16)
        if flip:
            folds = zero
            for t in range(s.tasks):
                folds = jnp.where(own == wide + t * s.width, 1.0, folds)
            mats[5] = folds.astype(jnp.bfloat16)
        factors_ref[flip] = factors.astype(jnp.bfloat16)
        if not flip:
            swap = jnp.where(jnp.logical_and(own == wide, own < s.feat), -2.0, zero)
            for i in range(PIECES):
                there = jnp.logical_and(own == s.one + i, wide == s.norm + i)
                back = jnp.logical_and(own == s.norm + i, wide == s.one + i)
                swap = jnp.where(jnp.logical_or(there, back), 1.0, swap)
            mats[0] = swap.astype(jnp.bfloat16)


def pack_points(s, points_ref, ids_ref, rhs_ref, scales_ref):
    n = points_ref.shape[1]
    scales = jnp.broadcast_to(scales_ref[...], (8, s.feat)).T[:, :1]
    scaled = (points_ref[...].astype(jnp.float32) / scales).astype(jnp.bfloat16)
    scaled = scaled.astype(jnp.float32)
    rest = jnp.sum(scaled * scaled, axis=0, keepdims=True)
    height = s.rhs - s.feat
    ids = ids_ref[...][None, :]
    row = lax.broadcasted_iota(jnp.int32, (height, n), 0) + s.feat
    extra = jnp.where(jnp.logical_and(row >= s.one, row < s.one + PIECES), 1.0, 0.0)
    for i in range(PIECES):
        top = rest.astype(jnp.bfloat16).astype(jnp.float32)
        extra = jnp.where(row == s.norm + i, top, extra)
        rest = rest - top
    for i in range(PIECES):
        extra = jnp.where(row - (s.hot + i * s.tasks) == ids, 1.0, extra)
    packed = jnp.concatenate([scaled, extra, rhs_ref[...].astype(jnp.float32)], axis=0)
    return packed.T.astype(jnp.bfloat16)


def matern(squared):
    squared = jnp.maximum(squared, 1e-30)
    root = squared * lax.rsqrt(squared)
    decay = jnp.exp2(root * (-math.sqrt(5.0) / math.log(2.0)))
    shaped = ((squared + 0.6) + root * (3.0 / math.sqrt(5.0))) * decay
    return shaped.astype(jnp.bfloat16)


def dot(left, right, dims=None):
    dims = dims or (((1,), (0,)), ((), ()))
    return lax.dot_general(left, right, dims, preferred_element_type=jnp.float32)


def kernel(
    s, low, n_strip, high,
    points_ref, ids_ref, rhs_ref, scales_ref, coregion_ref, noise_ref, out_ref,
    mats_ref, factors_ref, rows, cols, col_w, col_r, row_r, row_sums, col_sums,
    row_out, row_in, col_out, col_in,
    row_send, row_recv, col_send, col_recv, back_send, back_recv, side_send, side_recv,
):
    n = points_ref.shape[1]
    n_a, n_b = low * n_strip, high
    half_a, half_b = n_a // 2, n_b // 2
    blk, strip = lax.axis_index("blk"), lax.axis_index("strip")
    mine_b, mine_a = blk // low, (blk % low) * n_strip + strip

    def peer_a(index):
        return (mine_b * low + index // n_strip, index % n_strip)

    def peer_b(index):
        return (index * low + blk % low, strip)

    def copy(src, dst, send, recv, peer):
        return pltpu.make_async_remote_copy(
            src_ref=src, dst_ref=dst, send_sem=send, recv_sem=recv,
            device_id=peer, device_id_type=MESH,
        )

    def row_copy(k):
        return copy(
            rows.at[0], rows.at[k], row_send.at[k], row_recv.at[k], peer_a((mine_a + k) % n_a)
        )

    def col_copy(k):
        return copy(
            rows.at[0], cols.at[k], col_send.at[k], col_recv.at[k], peer_b((mine_b + k) % n_b)
        )

    def row_back(k):
        return copy(
            row_out.at[k], row_in.at[k], back_send.at[k], back_recv.at[k],
            peer_a((mine_a + n_a - k) % n_a),
        )

    def col_back(k):
        return copy(
            col_out.at[k], col_in.at[k], side_send.at[k], side_recv.at[k],
            peer_b((mine_b + n_b - k) % n_b),
        )

    barrier = pltpu.get_barrier_semaphore()
    for k in range(1, n_a):
        pl.semaphore_signal(
            barrier, inc=1, device_id=peer_a((mine_a + k) % n_a), device_id_type=MESH
        )
    for k in range(1, n_b):
        pl.semaphore_signal(
            barrier, inc=1, device_id=peer_b((mine_b + k) % n_b), device_id_type=MESH
        )
    mine = pack_points(s, points_ref, ids_ref, rhs_ref, scales_ref)
    rows[0] = mine
    cols[0] = mine
    build_mats(s, coregion_ref, mats_ref, factors_ref)
    row_sums[...] = jnp.zeros_like(row_sums)
    col_sums[...] = jnp.zeros_like(col_sums)
    pl.semaphore_wait(barrier, n_a + n_b - 2)

    for k in range(1, half_a + 1):
        row_copy(k).start()
    for gi in range(1, n_b):
        col_copy((gi + 1) // 2 if gi % 2 else n_b - gi // 2).start()


    def send_col(kb):
        total = col_sums[kb] * dot(factors_ref[1], cols[kb], NT)
        packed = total[:s.width]
        for i in range(1, s.tasks):
            packed = packed + total[i * s.width:(i + 1) * s.width]
        col_out[kb] = packed

        @pl.when(kb > 0)
        def _():
            col_back(kb).start()

    def group(gi, _):
        kb = jnp.where(gi % 2 == 1, (gi + 1) // 2, (n_b - gi // 2) % n_b)

        @pl.when(gi > 0)
        def _():
            col_copy(kb).wait_recv()

        block = cols[kb]
        col_w[...] = dot(block, mats_ref[0]).astype(jnp.bfloat16)
        col_r[...] = (dot(block, mats_ref[1]) * dot(block, mats_ref[2])).astype(jnp.bfloat16)

        def tile(t, _):
            ka = jnp.where(gi == 0, t, (t + 1) % (half_a + 1))

            @pl.when(gi == 0)
            def _():
                @pl.when(t > 0)
                def _():
                    row_copy(ka).wait_recv()

                block = rows[ka]
                row_r[ka] = (
                    dot(mats_ref[3], block, NT) * dot(mats_ref[4], block, NT)
                ).astype(jnp.bfloat16)

            alone = jnp.logical_and(
                jnp.logical_or(ka == 0, ka == half_a), jnp.logical_or(kb == 0, kb == half_b)
            )
            side = jnp.where(alone, n_b, kb)
            shaped = matern(dot(rows[ka], col_w[...], NT))
            row_sums[ka] = row_sums[ka] + dot(shaped, col_r[...])
            col_sums[side] = col_sums[side] + dot(row_r[ka], shaped)

            @pl.when(jnp.logical_and(gi == n_b - 1, ka == half_a - 1))
            def _():
                send_col(kb)

            @pl.when(gi == n_b - 1)
            def _():
                rest = row_sums[ka] * dot(rows[ka], factors_ref[0])
                packed = jnp.zeros((s.width, n), jnp.float32)
                for _ in range(PIECES):
                    top = rest.astype(jnp.bfloat16)
                    packed = packed + dot(mats_ref[5, :s.width, :], top, NT)
                    rest = rest - top.astype(jnp.float32)
                row_out[ka] = packed

                @pl.when(ka > 0)
                def _():
                    row_back(ka).start()

            return 0

        lax.fori_loop(0, jnp.where(kb <= half_b, half_a + 1, half_a - 1), tile, 0)
        @pl.when(gi < n_b - 1)
        def _():
            send_col(kb)

        return 0

    lax.fori_loop(0, n_b, group, 0)
    side = col_out[0]
    for k in range(1, n_b):
        col_back(k).wait_recv()
        side = side + col_in[k]
    side = side + row_out[0]
    for k in range(1, half_a + 1):
        row_back(k).wait_recv()
        side = side + row_in[k]
    out_ref[...] = side + noise_ref[0] * rhs_ref[...].astype(jnp.float32)
    for k in range(1, half_a + 1):
        row_copy(k).wait_send()
        row_back(k).wait_send()
    for k in range(1, n_b):
        col_copy(k).wait_send()
        col_back(k).wait_send()


def solution(mesh):
    n_blk, n_strip = mesh.shape["blk"], mesh.shape["strip"]
    low = low_size(n_blk, n_strip)
    high = n_blk // low
    n_a, n_b = low * n_strip, high
    assert n_a % 2 == 0 and n_b % 2 == 0 and n_a > 2
    half = n_a // 2 + 1

    def body(points, task_ids, rhs, length_scales, coregion, noise):
        n = points.shape[0]
        s = Sizes(points.shape[1], coregion.shape[0], rhs.shape[1])
        vmem = pl.BlockSpec(memory_space=pltpu.VMEM)
        smem = pl.BlockSpec(memory_space=pltpu.SMEM)
        bf16, f32 = jnp.bfloat16, jnp.float32
        return pl.pallas_call(
            functools.partial(kernel, s, low, n_strip, high),
            out_shape=jax.ShapeDtypeStruct((s.width, n), f32),
            in_specs=[vmem, vmem, vmem, vmem, smem, smem],
            out_specs=vmem,
            scratch_shapes=[
                pltpu.VMEM((6, LANES, LANES), bf16),
                pltpu.VMEM((2, LANES, LANES), bf16),
                pltpu.VMEM((half, n, LANES), bf16),
                pltpu.VMEM((n_b, n, LANES), bf16),
                pltpu.VMEM((n, LANES), bf16),
                pltpu.VMEM((n, LANES), bf16),
                pltpu.VMEM((half, LANES, n), bf16),
                pltpu.VMEM((half, n, LANES), f32),
                pltpu.VMEM((n_b + 1, LANES, n), f32),
                pltpu.VMEM((half, s.width, n), f32),
                pltpu.VMEM((half, s.width, n), f32),
                pltpu.VMEM((n_b, s.width, n), f32),
                pltpu.VMEM((n_b, s.width, n), f32),
                *[pltpu.SemaphoreType.DMA((half,))] * 2,
                *[pltpu.SemaphoreType.DMA((n_b,))] * 2,
                *[pltpu.SemaphoreType.DMA((half,))] * 2,
                *[pltpu.SemaphoreType.DMA((n_b,))] * 2,
            ],
            compiler_params=pltpu.CompilerParams(
                collective_id=0, has_side_effects=True, vmem_limit_bytes=24 * 1024 * 1024
            ),
        )(points.T, task_ids, rhs.T, length_scales[None, :], coregion, noise).T

    return jax.shard_map(
        body,
        mesh=mesh,
        in_specs=(
            P(("blk", "strip"), None),
            P(("blk", "strip")),
            P(("blk", "strip"), None),
            P(),
            P(),
            P(),
        ),
        out_specs=P(("blk", "strip"), None),
        check_vma=False,
    )
```

```python
import functools
import math

import jax
import jax.numpy as jnp
from jax import lax
from jax.experimental import pallas as pl
from jax.experimental.pallas import tpu as pltpu
from jax.sharding import PartitionSpec as P

MESH = pl.DeviceIdType.MESH
LANES = 128
NT = (((1,), (1,)), ((), ()))
PIECES = 3


def low_size(n_blk, n_strip):
    for size in range(1, n_blk + 1):
        if n_blk % size == 0 and size * n_strip >= n_blk // size:
            return size
    return n_blk


class Sizes:
    def __init__(self, feat, tasks, width):
        self.feat, self.tasks, self.width = feat, tasks, width
        self.norm = feat
        self.one = feat + PIECES
        self.hot = feat + 2 * PIECES
        self.rhs = LANES - width


def build_mats(s, coregion_ref, mats, factors_ref):
    for flip in (0, 1):
        own = lax.broadcasted_iota(jnp.int32, (LANES, LANES), flip)
        wide = lax.broadcasted_iota(jnp.int32, (LANES, LANES), 1 - flip)
        zero = jnp.zeros((LANES, LANES), jnp.float32)
        hots, vals, factors = zero, zero, zero
        for t in range(s.tasks):
            inside = jnp.logical_and(wide >= t * s.width, wide < (t + 1) * s.width)
            hots = jnp.where(jnp.logical_and(inside, own == s.hot + t), 1.0, hots)
            vals = jnp.where(jnp.logical_and(inside, own == wide + (s.rhs - t * s.width)), 1.0, vals)
            for b in range(s.tasks):
                rest = jnp.full((LANES, LANES), coregion_ref[b, t] * jnp.float32(5.0 / 3.0))
                for piece in range(PIECES):
                    top = rest.astype(jnp.bfloat16).astype(jnp.float32)
                    here = own == s.hot + piece * s.tasks + b
                    factors = jnp.where(jnp.logical_and(inside, here), top, factors)
                    rest = rest - top
        mats[1 + 2 * flip] = hots.astype(jnp.bfloat16)
        mats[2 + 2 * flip] = vals.astype(jnp.bfloat16)
        if flip:
            folds = zero
            for t in range(s.tasks):
                folds = jnp.where(own == wide + t * s.width, 1.0, folds)
            mats[5] = folds.astype(jnp.bfloat16)
        factors_ref[flip] = factors.astype(jnp.bfloat16)
        if not flip:
            swap = jnp.where(jnp.logical_and(own == wide, own < s.feat), -2.0, zero)
            for i in range(PIECES):
                there = jnp.logical_and(own == s.one + i, wide == s.norm + i)
                back = jnp.logical_and(own == s.norm + i, wide == s.one + i)
                swap = jnp.where(jnp.logical_or(there, back), 1.0, swap)
            mats[0] = swap.astype(jnp.bfloat16)


def pack_points(s, points_ref, ids_ref, rhs_ref, scales_ref):
    n = points_ref.shape[1]
    scales = jnp.broadcast_to(scales_ref[...], (8, s.feat)).T[:, :1]
    scaled = (points_ref[...].astype(jnp.float32) / scales).astype(jnp.bfloat16)
    scaled = scaled.astype(jnp.float32)
    rest = jnp.sum(scaled * scaled, axis=0, keepdims=True)
    height = s.rhs - s.feat
    ids = ids_ref[...][None, :]
    row = lax.broadcasted_iota(jnp.int32, (height, n), 0) + s.feat
    extra = jnp.where(jnp.logical_and(row >= s.one, row < s.one + PIECES), 1.0, 0.0)
    for i in range(PIECES):
        top = rest.astype(jnp.bfloat16).astype(jnp.float32)
        extra = jnp.where(row == s.norm + i, top, extra)
        rest = rest - top
    for i in range(PIECES):
        extra = jnp.where(row - (s.hot + i * s.tasks) == ids, 1.0, extra)
    packed = jnp.concatenate([scaled, extra, rhs_ref[...].astype(jnp.float32)], axis=0)
    return packed.T.astype(jnp.bfloat16)


def matern(squared):
    squared = jnp.maximum(squared, 1e-30)
    root = squared * lax.rsqrt(squared)
    decay = jnp.exp2(root * (-math.sqrt(5.0) / math.log(2.0)))
    shaped = ((squared + 0.6) + root * (3.0 / math.sqrt(5.0))) * decay
    return shaped.astype(jnp.bfloat16)


def dot(left, right, dims=None):
    dims = dims or (((1,), (0,)), ((), ()))
    return lax.dot_general(left, right, dims, preferred_element_type=jnp.float32)


def kernel(
    s, low, n_strip, high,
    points_ref, ids_ref, rhs_ref, scales_ref, coregion_ref, noise_ref, out_ref,
    mats_ref, factors_ref, rows, cols, col_w, col_r, row_r, row_sums, col_sums,
    row_out, row_in, col_out, col_in,
    row_send, row_recv, col_send, col_recv, back_send, back_recv, side_send, side_recv,
):
    n = points_ref.shape[1]
    n_a, n_b = low * n_strip, high
    half_a, half_b = n_a // 2, n_b // 2
    blk, strip = lax.axis_index("blk"), lax.axis_index("strip")
    mine_b, mine_a = blk // low, (blk % low) * n_strip + strip

    def peer_a(index):
        return (mine_b * low + index // n_strip, index % n_strip)

    def peer_b(index):
        return (index * low + blk % low, strip)

    def copy(src, dst, send, recv, peer):
        return pltpu.make_async_remote_copy(
            src_ref=src, dst_ref=dst, send_sem=send, recv_sem=recv,
            device_id=peer, device_id_type=MESH,
        )

    def row_copy(k):
        return copy(
            rows.at[0], rows.at[k], row_send.at[k], row_recv.at[k], peer_a((mine_a + k) % n_a)
        )

    def col_copy(k):
        return copy(
            rows.at[0], cols.at[k], col_send.at[k], col_recv.at[k], peer_b((mine_b + k) % n_b)
        )

    def row_back(k):
        return copy(
            row_out.at[k], row_in.at[k], back_send.at[k], back_recv.at[k],
            peer_a((mine_a + n_a - k) % n_a),
        )

    def col_back(k):
        return copy(
            col_out.at[k], col_in.at[k], side_send.at[k], side_recv.at[k],
            peer_b((mine_b + n_b - k) % n_b),
        )

    barrier = pltpu.get_barrier_semaphore()
    for k in range(1, n_a):
        pl.semaphore_signal(
            barrier, inc=1, device_id=peer_a((mine_a + k) % n_a), device_id_type=MESH
        )
    for k in range(1, n_b):
        pl.semaphore_signal(
            barrier, inc=1, device_id=peer_b((mine_b + k) % n_b), device_id_type=MESH
        )
    mine = pack_points(s, points_ref, ids_ref, rhs_ref, scales_ref)
    rows[0] = mine
    cols[0] = mine
    build_mats(s, coregion_ref, mats_ref, factors_ref)
    row_sums[...] = jnp.zeros_like(row_sums)
    col_sums[...] = jnp.zeros_like(col_sums)
    pl.semaphore_wait(barrier, n_a + n_b - 2)

    for k in range(1, half_a + 1):
        row_copy(k).start()
    for gi in range(1, n_b):
        col_copy((gi + 1) // 2 if gi % 2 else n_b - gi // 2).start()


    def send_col(kb):
        total = col_sums[kb] * dot(factors_ref[1], cols[kb], NT)
        packed = total[:s.width]
        for i in range(1, s.tasks):
            packed = packed + total[i * s.width:(i + 1) * s.width]
        col_out[kb] = packed

        @pl.when(kb > 0)
        def _():
            col_back(kb).start()

    def group(gi, _):
        kb = jnp.where(gi % 2 == 1, (gi + 1) // 2, (n_b - gi // 2) % n_b)

        @pl.when(gi > 0)
        def _():
            col_copy(kb).wait_recv()

        block = cols[kb]
        col_w[...] = dot(block, mats_ref[0]).astype(jnp.bfloat16)
        col_r[...] = (dot(block, mats_ref[1]) * dot(block, mats_ref[2])).astype(jnp.bfloat16)

        def tile(t, _):
            ka = jnp.where(gi == 0, t, (t + 1) % (half_a + 1))

            @pl.when(gi == 0)
            def _():
                @pl.when(t > 0)
                def _():
                    row_copy(ka).wait_recv()

                block = rows[ka]
                row_r[ka] = (
                    dot(mats_ref[3], block, NT) * dot(mats_ref[4], block, NT)
                ).astype(jnp.bfloat16)

            alone = jnp.logical_and(
                jnp.logical_or(ka == 0, ka == half_a), jnp.logical_or(kb == 0, kb == half_b)
            )
            side = jnp.where(alone, n_b, kb)
            shaped = matern(dot(rows[ka], col_w[...], NT))
            row_sums[ka] = row_sums[ka] + dot(shaped, col_r[...])
            col_sums[side] = col_sums[side] + dot(row_r[ka], shaped)

            @pl.when(jnp.logical_and(gi == n_b - 1, ka == half_a - 1))
            def _():
                send_col(kb)

            @pl.when(gi == n_b - 1)
            def _():
                rest = row_sums[ka] * dot(rows[ka], factors_ref[0])
                packed = jnp.zeros((s.width, n), jnp.float32)
                for _ in range(PIECES):
                    top = rest.astype(jnp.bfloat16)
                    packed = packed + dot(mats_ref[5, :s.width, :], top, NT)
                    rest = rest - top.astype(jnp.float32)
                row_out[ka] = packed

                @pl.when(ka > 0)
                def _():
                    row_back(ka).start()

            return 0

        lax.fori_loop(0, jnp.where(kb <= half_b, half_a + 1, half_a - 1), tile, 0)
        @pl.when(gi < n_b - 1)
        def _():
            send_col(kb)

        return 0

    lax.fori_loop(0, n_b, group, 0)
    side = col_out[0]
    for k in range(1, n_b):
        col_back(k).wait_recv()
        side = side + col_in[k]
    side = side + row_out[0]
    for k in range(1, half_a + 1):
        row_back(k).wait_recv()
        side = side + row_in[k]
    out_ref[...] = side + noise_ref[0] * rhs_ref[...].astype(jnp.float32)
    for k in range(1, half_a + 1):
        row_copy(k).wait_send()
        row_back(k).wait_send()
    for k in range(1, n_b):
        col_copy(k).wait_send()
        col_back(k).wait_send()


def solution(mesh):
    n_blk, n_strip = mesh.shape["blk"], mesh.shape["strip"]
    low = low_size(n_blk, n_strip)
    high = n_blk // low
    n_a, n_b = low * n_strip, high
    assert n_a % 2 == 0 and n_b % 2 == 0 and n_a > 2
    half = n_a // 2 + 1

    def body(points, task_ids, rhs, length_scales, coregion, noise):
        n = points.shape[0]
        s = Sizes(points.shape[1], coregion.shape[0], rhs.shape[1])
        vmem = pl.BlockSpec(memory_space=pltpu.VMEM)
        smem = pl.BlockSpec(memory_space=pltpu.SMEM)
        bf16, f32 = jnp.bfloat16, jnp.float32
        return pl.pallas_call(
            functools.partial(kernel, s, low, n_strip, high),
            out_shape=jax.ShapeDtypeStruct((s.width, n), f32),
            in_specs=[vmem, vmem, vmem, vmem, smem, smem],
            out_specs=vmem,
            scratch_shapes=[
                pltpu.VMEM((6, LANES, LANES), bf16),
                pltpu.VMEM((2, LANES, LANES), bf16),
                pltpu.VMEM((half, n, LANES), bf16),
                pltpu.VMEM((n_b, n, LANES), bf16),
                pltpu.VMEM((n, LANES), bf16),
                pltpu.VMEM((n, LANES), bf16),
                pltpu.VMEM((half, LANES, n), bf16),
                pltpu.VMEM((half, n, LANES), f32),
                pltpu.VMEM((n_b + 1, LANES, n), f32),
                pltpu.VMEM((half, s.width, n), f32),
                pltpu.VMEM((half, s.width, n), f32),
                pltpu.VMEM((n_b, s.width, n), f32),
                pltpu.VMEM((n_b, s.width, n), f32),
                *[pltpu.SemaphoreType.DMA((half,))] * 2,
                *[pltpu.SemaphoreType.DMA((n_b,))] * 2,
                *[pltpu.SemaphoreType.DMA((half,))] * 2,
                *[pltpu.SemaphoreType.DMA((n_b,))] * 2,
            ],
            compiler_params=pltpu.CompilerParams(
                collective_id=0, has_side_effects=True, vmem_limit_bytes=60000 * 1024
            ),
        )(points.T, task_ids, rhs.T, length_scales[None, :], coregion, noise).T

    return jax.shard_map(
        body,
        mesh=mesh,
        in_specs=(
            P(("blk", "strip"), None),
            P(("blk", "strip")),
            P(("blk", "strip"), None),
            P(),
            P(),
            P(),
        ),
        out_specs=P(("blk", "strip"), None),
        check_vma=False,
    )
```
